256 devices in a mesh: segment: 4 (over y), blk: 64 (over x, z, core).
Axes of the slice: x: 4, y: 4, z: 8, core: 2. Of those that a mesh axis runs over, the one named last changes fastest.
Arguments:
- inputs: bfloat16 [4, 1024, 64, 128], P(None, 'blk'), may hold values from -6 to 6
- weights: bfloat16 [8, 1024, 64, 2048], P('segment', 'blk'), may hold values from -0.1875 to 0.1875
- biases: float32 [8, 1024, 64], P('segment', 'blk'), may hold values from -3 to 3
- tile_index: int32 [8, 1024, 32], P('segment', 'blk'), may hold values from 0 to 31, each once within a row
Outputs:
- final_activity: bfloat16 [4, 1024, 64, 128], P('segment', 'blk')
The draws below stay inside these ranges and needn't reach their ends.
Inputs may be any that keep to these rules, and one draw needn't show every extreme that they name: `tile_index`: each row of 32 entries names every member 0..31 once.
All inputs are finite; a program needn't handle non-finite values.
Results may differ from the reference program's by a relative error of at most 0.014.
Values may be sent and summed in bfloat16 or wider, within the bound.
A program may use at most 128 MiB of HBM per device.

```python
import jax
import jax.numpy as jnp
from jax import lax

TILE = 64
FANIN = 32
BATCH = 128
BLK_DEV = 16
BLOCKS = 1024
GRP = 16
OUTER = 1
LAYERS = 8
MB = 4


def steps_of(key, extent, pieces, smallest, largest):
    def one(position, shards_of):
        draws = jax.random.uniform(jax.random.fold_in(jax.random.fold_in(key, 6), position), (shards_of,), jnp.float32, smallest / len(pieces), largest / len(pieces))
        return jnp.repeat(jnp.exp(draws), extent[position] // shards_of).reshape((-1,) + (1,) * (len(extent) - position - 1))

    level = one(*pieces[0])
    for cut in pieces[1:]:
        level = level * one(*cut)
    return level


def gaussian(stream_key, shape, width, reach, pieces=(), kind=jnp.bfloat16):
    drawn = width * jax.random.normal(stream_key, shape, jnp.float32)
    if pieces:
        drawn = drawn * steps_of(stream_key, shape, pieces, -0.22, 0.18)
    return jnp.clip(drawn, -reach, reach).astype(kind)


def setup_inputs(seed: int = 0) -> dict:
    streams_of = jax.random.split(jax.random.key(seed), 5)
    inputs = gaussian(streams_of[0], (MB, BLOCKS, TILE, BATCH), 1.0, 6.0, ((1, 64),))
    weights = gaussian(streams_of[1], (LAYERS, BLOCKS, TILE, FANIN * TILE), (FANIN * TILE // 2) ** -0.5, 0.1875, ((0, 4), (1, 64)))
    biases = gaussian(streams_of[2], (LAYERS, BLOCKS, TILE), 0.5, 3.0, ((0, 4), (1, 64)), jnp.float32)
    tile_index = jax.vmap(lambda own: jax.random.permutation(own, FANIN))(jax.random.split(streams_of[3], LAYERS * BLOCKS)).reshape((LAYERS, BLOCKS, FANIN)).astype(jnp.int32)
    return {"inputs": inputs, "weights": weights, "biases": biases, "tile_index": tile_index}


def group_layer(values, weight_groups, bias_groups, index_groups):
    def one_group(packed):
        group_values, group_weights, group_biases, group_index = packed
        onehot = (group_index[:, :, None] == jnp.arange(FANIN, dtype=jnp.int32)[None, None, :]).astype(jnp.float32)
        shaped = group_weights.astype(jnp.float32).reshape(FANIN, TILE, FANIN, TILE)
        placed = jnp.einsum("jakc,jkm->jamc", shaped, onehot, precision=lax.Precision.HIGHEST)
        placed = placed.reshape(FANIN * TILE, FANIN * TILE)
        flat_group = group_values.astype(jnp.float32).reshape(FANIN * TILE, -1)
        summed = jnp.dot(placed, flat_group, precision=lax.Precision.HIGHEST).reshape(FANIN, TILE, -1)
        summed = summed + group_biases[:, :, None]
        return jnp.maximum(summed, 0.0).astype(jnp.bfloat16)

    return lax.map(one_group, (values, weight_groups, bias_groups, index_groups))


def swap_digits(values):
    rest = values.shape[1:]
    shaped = values.reshape((OUTER * 2, GRP, 2, BLK_DEV // GRP, GRP) + rest)
    order = (0, 4, 2, 3, 1) + tuple(range(5, 5 + len(rest)))
    return shaped.transpose(order).reshape(values.shape)


def odd_groups(values):
    rest = values.shape[1:]
    shaped = values.reshape((OUTER, 2, GRP, 2, BLK_DEV) + rest)
    order = (0, 2, 3, 1, 4) + tuple(range(5, 5 + len(rest)))
    return shaped.transpose(order).reshape((BLOCKS // FANIN, FANIN) + rest)


def odd_ungroup(grouped):
    rest = grouped.shape[2:]
    shaped = grouped.reshape((OUTER, GRP, 2, 2, BLK_DEV) + rest)
    order = (0, 3, 1, 2, 4) + tuple(range(5, 5 + len(rest)))
    return shaped.transpose(order).reshape((BLOCKS,) + rest)


def even_groups(values):
    return values.reshape((BLOCKS // FANIN, FANIN) + values.shape[1:])


def reference(inputs, weights, biases, tile_index):
    values = jnp.transpose(inputs, (1, 2, 0, 3)).reshape(BLOCKS, TILE, MB * BATCH)
    for layer_index in range(LAYERS):
        if layer_index % 2 == 0:
            grouped = group_layer(even_groups(values), even_groups(weights[layer_index]),
                                  even_groups(biases[layer_index]), even_groups(tile_index[layer_index]))
            values = grouped.reshape(BLOCKS, TILE, MB * BATCH)
        else:
            swapped = swap_digits(values)
            grouped = group_layer(odd_groups(swapped), odd_groups(weights[layer_index]),
                                  odd_groups(biases[layer_index]), odd_groups(tile_index[layer_index]))
            values = swap_digits(odd_ungroup(grouped))
    return values.reshape(BLOCKS, TILE, MB, BATCH).transpose(2, 0, 1, 3)
```

```python
import functools

import jax
import jax.numpy as jnp
from jax import lax
from jax.experimental import pallas as pl
from jax.experimental.pallas import tpu as pltpu
from jax.sharding import PartitionSpec as P

MESH = pl.DeviceIdType.MESH
TILE = 64
HALF = 32
FANIN = 32
LANES = 128
SLOTS = 16
ZS = 8
XS = 4
SEGS = 4
MB = 4
CHUNKS = 2 * MB
LAYERS = 2
COLUMNS = FANIN // 2


def device(segment, x, z, core):
    return {"segment": segment, "blk": (x * ZS + z) * 2 + core}


def low_lanes(shape, width, period):
    lane = lax.broadcasted_iota(jnp.int32, shape, len(shape) - 1)
    return lax.rem(lane, period) < width


def repack(upper, lower):
    low = low_lanes(upper.shape, 64, 128)
    first = jnp.where(low, upper, pltpu.roll(lower, 64, upper.ndim - 1))
    second = jnp.where(low, pltpu.roll(upper, 64, upper.ndim - 1), lower)
    return first, second


def kernel(
    source, weights, bias, inputs, out,
    raw_even, raw_odd, near, far, entering, hidden, landed, odd_in, leaving, final, staged,
    raw_sem, in_sem, entry_recv, entry_send, core_recv, core_send, z_recv, z_send, z_own,
    x_recv, x_send, x_own, final_recv, final_own,
):
    raw = (raw_even, raw_odd)
    segment = lax.axis_index("segment")
    position = lax.axis_index("blk")
    x, z, core = position // (2 * ZS), position // 2 % ZS, position % 2
    upper, inner = x // 2, x % 2
    pair = device(segment, x, z, 1 - core)
    last = segment == SEGS - 1
    first = segment == 0

    def remote(src, dst, send, recv, target):
        return pltpu.make_async_remote_copy(
            src_ref=src, dst_ref=dst, send_sem=send, recv_sem=recv,
            device_id=target, device_id_type=MESH,
        )

    barrier = pltpu.get_barrier_semaphore()

    def greet(target):
        pl.semaphore_signal(barrier, inc=1, device_id=target, device_id_type=MESH)

    greet(pair)
    for step in (2, 1, 3):
        greet(device(segment, (x + step) % XS, z, core))
    for step in (4, 3, 5, 2, 6, 1, 7):
        greet(device(segment, x, (z + step) % ZS, core))

    @pl.when(segment > 0)
    def _():
        for step in (4, 3, 5, 2, 6, 1, 7, 0):
            for other in range(2):
                greet(device(segment - 1, 2 * upper + other, (z + step) % ZS, core))

    def raw_start(layer):
        for column in range(COLUMNS):
            pltpu.make_async_copy(
                weights.at[layer, :, :, pl.ds(column * LANES, LANES)],
                raw[layer].at[0, :, column], raw_sem.at[layer],
            ).start()

    def raw_copy(layer):
        return pltpu.make_async_copy(raw[layer].at[1], raw[layer].at[0], raw_sem.at[layer])

    def in_copy(batch):
        return pltpu.make_async_copy(inputs.at[batch], staged.at[batch], in_sem.at[batch])

    raw_start(0)

    @pl.when(first)
    def _():
        for batch in range(MB):
            in_copy(batch).start()

    raw_start(1)

    def arrange(layer):
        tiles = raw[layer]
        raw_copy(layer).wait()

        def turn(slot, carry):
            for column in range(COLUMNS):
                tiles[1, slot, column] = pltpu.roll(tiles[0, slot, column], 64, 1)
            return carry

        lax.fori_loop(0, SLOTS, turn, 0)

        def one_slot(slot, carry):
            row = (layer * SLOTS + slot) * FANIN
            rows = pl.ds(pl.multiple_of(slot * TILE, TILE), TILE)
            low = low_lanes((TILE, LANES), 64, 128)
            quarter = low_lanes((TILE, LANES), 32, 64)

            def tile_at(member, half):
                tile = source[row + member]
                return tiles[(tile + half) % 2, slot, tile // 2]

            for quad in range(FANIN // 4):
                even = jnp.where(low, tile_at(4 * quad, 0), tile_at(4 * quad + 2, 1))
                odd = jnp.where(low, tile_at(4 * quad + 1, 0), tile_at(4 * quad + 3, 1))
                lanes = pl.ds(quad * LANES, LANES)
                near[layer, rows, lanes] = jnp.where(quarter, even, pltpu.roll(odd, 32, 1))
                far[layer, rows, lanes] = jnp.where(quarter, pltpu.roll(even, 96, 1), odd)
            return carry

        lax.fori_loop(0, SLOTS, one_slot, 0)

    arrange(0)

    @pl.when(first)
    def _():
        for batch in range(MB):
            in_copy(batch).wait()

        def pack(step, carry):
            batch, block = step // SLOTS, step % SLOTS
            one, two = repack(
                staged[batch, block, pl.ds(0, HALF), :], staged[batch, block, pl.ds(HALF, HALF), :]
            )
            entering[2 * batch, core, block] = one
            entering[2 * batch + 1, core, block] = two
            return carry

        lax.fori_loop(0, MB * SLOTS, pack, 0)

    pl.semaphore_wait(barrier, 11 + jnp.where(last, 0, 16))

    low = low_lanes((HALF, LANES), 64, 128)

    def multiply(layer, values, block, store):
        rows = pl.ds(pl.multiple_of(block * 4 * TILE, 4 * TILE), 4 * TILE)
        one = jnp.dot(near[layer, rows, :], values, preferred_element_type=jnp.float32)
        two = jnp.dot(far[layer, rows, :], values, preferred_element_type=jnp.float32)
        for slot in range(4):
            a, b, c = slot * TILE, slot * TILE + HALF, (slot + 1) * TILE
            kept = jnp.where(low, one[a:b], two[b:c])
            moved = jnp.where(low, one[b:c], two[a:b])
            total = kept + pltpu.roll(moved, 64, 1) + bias[layer, block * 4 + slot]
            store(slot, jnp.maximum(total, 0.0).astype(jnp.bfloat16))

    def core_copy(chunk):
        return remote(
            entering.at[chunk, core], entering.at[chunk, core],
            core_send.at[chunk], core_recv.at[chunk], pair,
        )

    def entry_done(chunk):
        return remote(
            leaving.at[chunk], entering.at[chunk, core],
            entry_send.at[chunk], entry_recv.at[chunk], pair,
        )

    def z_done(chunk):
        span = pl.ds(0, ZS - 1)
        return remote(
            hidden.at[chunk, :, span], landed.at[chunk, :, span],
            z_send.at[chunk], z_recv.at[chunk], pair,
        )

    def z_local(chunk):
        return pltpu.make_async_copy(
            hidden.at[chunk, :, z], landed.at[chunk, :, z], z_own.at[chunk]
        )

    def x_local(chunk):
        return pltpu.make_async_copy(
            landed.at[chunk, inner], odd_in.at[chunk, x], x_own.at[chunk]
        )

    def x_done(chunk):
        span = pl.ds(0, XS - 1)
        return remote(
            odd_in.at[chunk, span], odd_in.at[chunk, span],
            x_send.at[chunk], x_recv.at[chunk], pair,
        )

    def even_layer(chunk):
        @pl.when(segment > 0)
        def _():
            entry_done(chunk).wait_recv()

        core_copy(chunk).start()
        core_copy(chunk).wait_recv()
        values = entering[chunk].reshape(FANIN * HALF, LANES)
        for turn in range(2):
            part = (z // 4 + 1 + turn) % 2
            for other in range(2):
                def store(slot, block):
                    hidden[chunk, other, part * 4 + slot] = block

                multiply(0, values, 2 * other + part, store)
            for step in range(4):
                to = part * 4 + step

                @pl.when(to != z)
                def _():
                    remote(
                        hidden.at[chunk, :, to], landed.at[chunk, :, z],
                        z_send.at[chunk], z_recv.at[chunk], device(segment, x, to, core),
                    ).start()

                @pl.when(to == z)
                def _():
                    z_local(chunk).start()

    def spread(chunk):
        z_local(chunk).wait()
        z_done(chunk).wait_recv()
        for step in (2, 1, 3):
            to = (x + step) % XS
            remote(
                landed.at[chunk, to % 2], odd_in.at[chunk, x],
                x_send.at[chunk], x_recv.at[chunk], device(segment, to, z, core),
            ).start()
        x_local(chunk).start()

    def odd_layer(chunk):
        x_local(chunk).wait()
        x_done(chunk).wait_recv()
        values = odd_in[chunk].reshape(FANIN * HALF, LANES)
        goal = chunk // 2
        for turn in range(2):
            part = (z // 4 + 1 + turn) % 2
            for other in range(2):
                def store(slot, block):
                    leaving[chunk, other, part * 4 + slot] = block

                multiply(1, values, 2 * other + part, store)
                for step in range(4):
                    to = part * 4 + step
                    block = leaving.at[chunk, other, to]

                    @pl.when(segment < SEGS - 1)
                    def _():
                        remote(
                            block, entering.at[chunk, core, inner * ZS + z],
                            entry_send.at[chunk], entry_recv.at[chunk],
                            device(segment + 1, 2 * upper + other, to, core),
                        ).start()

                    @pl.when(last)
                    def _():
                        stays = (goal == SEGS - 1) & (to == z) & (other == inner)

                        @pl.when(jnp.logical_not(stays))
                        def _():
                            remote(
                                block, final.at[chunk % 2, inner * ZS + z],
                                entry_send.at[chunk], final_recv.at[chunk % 2],
                                device(goal, 2 * upper + other, to, core),
                            ).start()

                        @pl.when(stays)
                        def _():
                            pltpu.make_async_copy(
                                block, final.at[chunk % 2, inner * ZS + z],
                                final_own.at[chunk % 2],
                            ).start()

    def step(index, carry):
        @pl.when(index < CHUNKS)
        def _():
            even_layer(index)

        @pl.when(index == 0)
        def _():
            arrange(1)

        @pl.when(index > 0)
        def _():
            odd_layer(index - 1)

        @pl.when(index < CHUNKS)
        def _():
            spread(index)

        return carry

    lax.fori_loop(0, CHUNKS + 1, step, 0)

    def final_done(half, count):
        span = pl.ds(0, count)
        return remote(
            final.at[half, span], final.at[half, span],
            entry_send.at[half], final_recv.at[half], pair,
        )

    @pl.when(segment < SEGS - 1)
    def _():
        for half in range(2):
            final_done(half, SLOTS).wait_recv()

    @pl.when(last)
    def _():
        for half in range(2):
            final_done(half, SLOTS - 1).wait_recv()
            pltpu.make_async_copy(final.at[half, 0], final.at[half, 0], final_own.at[half]).wait()

    def unpack(block, carry):
        one, two = repack(final[0, block], final[1, block])
        out[block, pl.ds(0, HALF), :] = one
        out[block, pl.ds(HALF, HALF), :] = two
        return carry

    lax.fori_loop(0, SLOTS, unpack, 0)

    def drain(chunk, carry):
        core_copy(chunk).wait_send()
        z_done(chunk).wait_send()
        x_done(chunk).wait_send()
        whole = jnp.logical_not(last & (chunk // 2 == SEGS - 1))

        @pl.when(whole)
        def _():
            entry_done(chunk).wait_send()

        @pl.when(jnp.logical_not(whole))
        def _():
            span = pl.ds(0, SLOTS - 1)
            remote(
                final.at[0, span], final.at[0, span],
                entry_send.at[chunk], final_recv.at[0], pair,
            ).wait_send()

        return carry

    lax.fori_loop(0, CHUNKS, drain, 0)


def body(inputs, weights, biases, tile_index):
    order = jnp.arange(FANIN, dtype=jnp.int32)
    source = jnp.sum(
        jnp.where(tile_index[..., :, None] == order, order[:, None], 0), axis=-2, dtype=jnp.int32
    )
    parts = biases.reshape(LAYERS, SLOTS, 2, HALF).transpose(0, 1, 3, 2)
    bias = jnp.broadcast_to(parts[..., None], (LAYERS, SLOTS, HALF, 2, LANES // 2))
    bias = bias.reshape(LAYERS, SLOTS, HALF, LANES)
    dma = pltpu.SemaphoreType.DMA
    packed = (HALF, LANES)
    vmem = lambda *shape: pltpu.VMEM(shape, jnp.bfloat16)
    result = pl.pallas_call(
        kernel,
        out_shape=jax.ShapeDtypeStruct((SLOTS, TILE, LANES), jnp.bfloat16),
        in_specs=[
            pl.BlockSpec(memory_space=pltpu.SMEM),
            pl.BlockSpec(memory_space=pl.ANY),
            pl.BlockSpec(memory_space=pltpu.VMEM),
            pl.BlockSpec(memory_space=pl.ANY),
        ],
        out_specs=pl.BlockSpec(memory_space=pltpu.VMEM),
        scratch_shapes=[
            vmem(2, SLOTS, COLUMNS, TILE, LANES),
            vmem(2, SLOTS, COLUMNS, TILE, LANES),
            vmem(LAYERS, SLOTS * TILE, FANIN * HALF),
            vmem(LAYERS, SLOTS * TILE, FANIN * HALF),
            vmem(CHUNKS, 2, SLOTS, *packed),
            vmem(CHUNKS, 2, ZS, *packed),
            vmem(CHUNKS, 2, ZS, *packed),
            vmem(CHUNKS, XS, ZS, *packed),
            vmem(CHUNKS, 2, ZS, *packed),
            vmem(2, SLOTS, *packed),
            vmem(MB, SLOTS, TILE, LANES),
            dma((LAYERS,)),
            dma((MB,)),
        ]
        + [dma((CHUNKS,))] * 10
        + [dma((2,)), dma((2,))],
        compiler_params=pltpu.CompilerParams(
            has_side_effects=True, collective_id=0, vmem_limit_bytes=60 * 1024 * 1024
        ),
    )(source.reshape(-1), weights, bias, inputs)
    return result[None]


def solution(mesh):
    in_specs = (
        P(None, "blk", None, None),
        P("segment", "blk", None, None),
        P("segment", "blk", None),
        P("segment", "blk", None),
    )
    out_specs = P("segment", "blk", None, None)
    return jax.shard_map(body, mesh=mesh, in_specs=in_specs, out_specs=out_specs, check_vma=False)
```

```python
import functools

import jax
import jax.numpy as jnp
from jax import lax
from jax.experimental import pallas as pl
from jax.experimental.pallas import tpu as pltpu
from jax.sharding import PartitionSpec as P

MESH = pl.DeviceIdType.MESH
TILE = 64
HALF = 32
FANIN = 32
LANES = 128
SLOTS = 16
ZS = 8
XS = 4
SEGS = 4
MB = 4
CHUNKS = 2 * MB
LAYERS = 2
ORDER = (("enter", 0), ("even", 0), ("spread", 1), ("odd", 2))
COLUMNS = FANIN // 2


def device(segment, x, z, core):
    return {"segment": segment, "blk": (x * ZS + z) * 2 + core}


def low_lanes(shape, width, period):
    lane = lax.broadcasted_iota(jnp.int32, shape, len(shape) - 1)
    return lax.rem(lane, period) < width


def repack(upper, lower):
    low = low_lanes(upper.shape, 64, 128)
    first = jnp.where(low, upper, pltpu.roll(lower, 64, upper.ndim - 1))
    second = jnp.where(low, pltpu.roll(upper, 64, upper.ndim - 1), lower)
    return first, second


def kernel(
    source, weights, bias_rows, inputs, out,
    raw_even, raw_odd, bias, near, far, entering, hidden, landed, odd_in, leaving, final, staged,
    raw_sem, in_sem, entry_recv, entry_send, core_recv, core_send, z_recv, z_send,
    x_recv, x_send, final_recv,
):
    raw = (raw_even, raw_odd)
    segment = lax.axis_index("segment")
    position = lax.axis_index("blk")
    x, z, core = position // (2 * ZS), position // 2 % ZS, position % 2
    upper, inner = x // 2, x % 2
    pair = device(segment, x, z, 1 - core)
    last = segment == SEGS - 1
    first = segment == 0

    def remote(src, dst, send, recv, target):
        return pltpu.make_async_remote_copy(
            src_ref=src, dst_ref=dst, send_sem=send, recv_sem=recv,
            device_id=target, device_id_type=MESH,
        )

    barrier = pltpu.get_barrier_semaphore()

    def greet(target):
        pl.semaphore_signal(barrier, inc=1, device_id=target, device_id_type=MESH)

    greet(pair)
    for step in (2, 1, 3):
        greet(device(segment, (x + step) % XS, z, core))
    for step in (4, 3, 5, 2, 6, 1, 7):
        greet(device(segment, x, (z + step) % ZS, core))

    @pl.when(segment > 0)
    def _():
        for step in (4, 3, 5, 2, 6, 1, 7, 0):
            for other in range(2):
                greet(device(segment - 1, 2 * upper + other, (z + step) % ZS, core))

    def raw_start(layer):
        for column in range(COLUMNS):
            pltpu.make_async_copy(
                weights.at[layer, :, :, pl.ds(column * LANES, LANES)],
                raw[layer].at[:, column], raw_sem.at[layer],
            ).start()

    def raw_copy(layer):
        return pltpu.make_async_copy(
            raw[layer].at[:, pl.ds(COLUMNS, COLUMNS)], raw[layer].at[:, pl.ds(0, COLUMNS)],
            raw_sem.at[layer],
        )

    def in_copy(batch):
        return pltpu.make_async_copy(inputs.at[batch], staged.at[batch], in_sem.at[batch])

    raw_start(0)

    @pl.when(first)
    def _():
        for batch in range(MB):
            in_copy(batch).start()

    raw_start(1)

    def arrange(layer):
        tiles = raw[layer]
        raw_copy(layer).wait()

        def turn(slot, carry):
            for column in range(COLUMNS):
                tiles[slot, COLUMNS + column] = pltpu.roll(tiles[slot, column], 64, 1)
            return carry

        lax.fori_loop(0, SLOTS, turn, 0)

        def one_slot(slot, carry):
            rows = pl.ds(pl.multiple_of(slot * TILE, TILE), TILE)
            low = low_lanes((TILE, LANES), 64, 128)
            quarter = low_lanes((TILE, LANES), 32, 64)
            ours = tiles.at[slot]

            def tile_at(member):
                return ours[source[layer, slot, member]]

            for quad in range(FANIN // 4):
                even = jnp.where(low, tile_at(4 * quad), tile_at(4 * quad + 2))
                odd = jnp.where(low, tile_at(4 * quad + 1), tile_at(4 * quad + 3))
                near[layer, quad, rows] = jnp.where(quarter, even, pltpu.roll(odd, 32, 1))
                far[layer, quad, rows] = jnp.where(quarter, pltpu.roll(even, 96, 1), odd)
            return carry

        lax.fori_loop(0, SLOTS, one_slot, 0)

    low = low_lanes((HALF, LANES), 64, 128)
    for layer in range(LAYERS):
        columns = jnp.transpose(bias_rows[layer], (1, 0))
        for slot in range(SLOTS):
            upper_half = jnp.broadcast_to(columns[:HALF, slot : slot + 1], (HALF, LANES))
            lower_half = jnp.broadcast_to(columns[HALF:, slot : slot + 1], (HALF, LANES))
            bias[layer, slot] = jnp.where(low, upper_half, lower_half)

    arrange(0)

    @pl.when(first)
    def _():
        for batch in range(MB):
            in_copy(batch).wait()

        def pack(step, carry):
            batch, block = step // SLOTS, step % SLOTS
            one, two = repack(
                staged[batch, block, pl.ds(0, HALF), :], staged[batch, block, pl.ds(HALF, HALF), :]
            )
            entering[2 * batch, core, block // ZS, block % ZS] = one
            entering[2 * batch + 1, core, block // ZS, block % ZS] = two
            return carry

        lax.fori_loop(0, MB * SLOTS, pack, 0)

    @pl.when(segment > 0)
    def _():
        arrange(1)

    pl.semaphore_wait(barrier, 11 + jnp.where(last, 0, 16))

    def joined(blocks, layer, rows):
        return jnp.concatenate([blocks[layer, quad, rows] for quad in range(FANIN // 4)], axis=1)

    def multiply(layer, values, block, store):
        rows = pl.ds(pl.multiple_of(block * 4 * TILE, 4 * TILE), 4 * TILE)
        one = jnp.dot(joined(near, layer, rows), values, preferred_element_type=jnp.float32)
        two = jnp.dot(joined(far, layer, rows), values, preferred_element_type=jnp.float32)
        for slot in range(4):
            a, b, c = slot * TILE, slot * TILE + HALF, (slot + 1) * TILE
            kept = jnp.where(low, one[a:b], two[b:c])
            moved = jnp.where(low, one[b:c], two[a:b])
            total = kept + pltpu.roll(moved, 64, 1) + bias[layer, block * 4 + slot]
            store(slot, jnp.maximum(total, 0.0).astype(jnp.bfloat16))

    def quarter_of(group):
        return pl.ds((z // 4 + 1 + group) % 2 * 4, 4)

    def core_copy(chunk, span):
        return remote(
            entering.at[chunk, core, :, span], entering.at[chunk, core, :, span],
            core_send.at[chunk], core_recv.at[chunk], pair,
        )

    def entry_done(chunk, group):
        span = pl.ds(0, 4)
        return remote(
            leaving.at[chunk, :, span], entering.at[chunk, core, :, span],
            entry_send.at[chunk], entry_recv.at[chunk, group], pair,
        )

    def z_done(chunk, group, count):
        span = pl.ds(0, count)
        return remote(
            hidden.at[chunk, :, span], landed.at[chunk, :, span],
            z_send.at[chunk], z_recv.at[chunk, group], pair,
        )

    def x_done(chunk):
        span = pl.ds(0, XS - 1)
        return remote(
            odd_in.at[chunk, span], odd_in.at[chunk, span],
            x_send.at[chunk], x_recv.at[chunk], pair,
        )

    def enter(chunk):
        for group in range(2):
            @pl.when(segment > 0)
            def _():
                entry_done(chunk, group).wait_recv()

            core_copy(chunk, quarter_of(group)).start()

    def even_layer(chunk):
        core_copy(chunk, pl.ds(0, ZS)).wait_recv()
        values = entering[chunk].reshape(FANIN * HALF, LANES)
        for group in range(2):
            part = (z // 4 + 1 + group) % 2
            for other in range(2):
                def store(slot, block):
                    hidden[chunk, other, part * 4 + slot] = block

                multiply(0, values, 2 * other + part, store)
            for step in range(4):
                to = part * 4 + step

                @pl.when(to != z)
                def _():
                    remote(
                        hidden.at[chunk, :, to], landed.at[chunk, :, z],
                        z_send.at[chunk], z_recv.at[chunk, group],
                        device(segment, x, to, core),
                    ).start()

    def spread(chunk):
        for group in range(2):
            z_done(chunk, group, 4 - group).wait_recv()
            if group == 1:
                landed[chunk, :, z] = hidden[chunk, :, z]
            span = quarter_of(group)
            for step in (2, 1, 3):
                to = (x + step) % XS
                remote(
                    landed.at[chunk, to % 2, span], odd_in.at[chunk, x, span],
                    x_send.at[chunk], x_recv.at[chunk], device(segment, to, z, core),
                ).start()
        odd_in[chunk, x] = landed[chunk, inner]

    def odd_layer(chunk):
        x_done(chunk).wait_recv()
        values = odd_in[chunk].reshape(FANIN * HALF, LANES)
        goal = chunk // 2
        for group in range(2):
            part = (z // 4 + 1 + group) % 2
            for other in range(2):
                def store(slot, block):
                    leaving[chunk, other, part * 4 + slot] = block

                multiply(1, values, 2 * other + part, store)
                for step in range(4):
                    to = part * 4 + step
                    block = leaving.at[chunk, other, to]

                    @pl.when(segment < SEGS - 1)
                    def _():
                        remote(
                            block, entering.at[chunk, core, inner, z],
                            entry_send.at[chunk], entry_recv.at[chunk, group],
                            device(segment + 1, 2 * upper + other, to, core),
                        ).start()

                    @pl.when(last)
                    def _():
                        stays = (goal == SEGS - 1) & (to == z) & (other == inner)

                        @pl.when(jnp.logical_not(stays))
                        def _():
                            remote(
                                block, final.at[chunk % 2, inner * ZS + z],
                                entry_send.at[chunk], final_recv.at[chunk % 2],
                                device(goal, 2 * upper + other, to, core),
                            ).start()

        @pl.when(last & (goal == SEGS - 1))
        def _():
            final[chunk % 2, inner * ZS + z] = leaving[chunk, inner, z]

    phases = {"enter": enter, "even": even_layer, "spread": spread, "odd": odd_layer}

    def step(index, carry):
        for name, lag in ORDER:
            chunk = index - lag

            @pl.when((chunk >= 0) & (chunk < CHUNKS))
            def _():
                phases[name](chunk)

            if name == "even":
                @pl.when(first & (chunk == 0))
                def _():
                    arrange(1)

        return carry

    lax.fori_loop(0, CHUNKS + max(lag for _, lag in ORDER), step, 0)

    def final_done(half, count):
        span = pl.ds(0, count)
        return remote(
            final.at[half, span], final.at[half, span],
            entry_send.at[half], final_recv.at[half], pair,
        )

    @pl.when(segment < SEGS - 1)
    def _():
        for half in range(2):
            final_done(half, SLOTS).wait_recv()

    @pl.when(last)
    def _():
        for half in range(2):
            final_done(half, SLOTS - 1).wait_recv()

    def unpack(block, carry):
        one, two = repack(final[0, block], final[1, block])
        out[block, pl.ds(0, HALF), :] = one
        out[block, pl.ds(HALF, HALF), :] = two
        return carry

    lax.fori_loop(0, SLOTS, unpack, 0)

    def drain(chunk, carry):
        core_copy(chunk, pl.ds(0, ZS)).wait_send()
        z_done(chunk, 0, ZS - 1).wait_send()
        x_done(chunk).wait_send()
        whole = jnp.logical_not(last & (chunk // 2 == SEGS - 1))

        @pl.when(whole)
        def _():
            span = pl.ds(0, SLOTS)
            remote(
                final.at[0, span], final.at[0, span],
                entry_send.at[chunk], final_recv.at[0], pair,
            ).wait_send()

        @pl.when(jnp.logical_not(whole))
        def _():
            span = pl.ds(0, SLOTS - 1)
            remote(
                final.at[0, span], final.at[0, span],
                entry_send.at[chunk], final_recv.at[0], pair,
            ).wait_send()

        return carry

    lax.fori_loop(0, CHUNKS, drain, 0)


def body(inputs, weights, biases, tile_index):
    order = jnp.arange(FANIN, dtype=jnp.int32)
    high = (order // 2) % 2
    place = (order[:, None] + high) % 2 * COLUMNS + order[:, None] // 2
    source = jnp.sum(
        jnp.where(tile_index[..., :, None] == order, place, 0), axis=-2, dtype=jnp.int32
    )
    dma = pltpu.SemaphoreType.DMA
    packed = (HALF, LANES)
    vmem = lambda *shape: pltpu.VMEM(shape, jnp.bfloat16)
    result = pl.pallas_call(
        kernel,
        out_shape=jax.ShapeDtypeStruct((SLOTS, TILE, LANES), jnp.bfloat16),
        in_specs=[
            pl.BlockSpec(memory_space=pltpu.SMEM),
            pl.BlockSpec(memory_space=pl.ANY),
            pl.BlockSpec(memory_space=pltpu.VMEM),
            pl.BlockSpec(memory_space=pl.ANY),
        ],
        out_specs=pl.BlockSpec(memory_space=pltpu.VMEM),
        scratch_shapes=[
            vmem(SLOTS, 2 * COLUMNS, TILE, LANES),
            vmem(SLOTS, 2 * COLUMNS, TILE, LANES),
            pltpu.VMEM((LAYERS, SLOTS, HALF, LANES), jnp.float32),
            vmem(LAYERS, FANIN // 4, SLOTS * TILE, LANES),
            vmem(LAYERS, FANIN // 4, SLOTS * TILE, LANES),
            vmem(CHUNKS, 2, 2, ZS, *packed),
            vmem(CHUNKS, 2, ZS, *packed),
            vmem(CHUNKS, 2, ZS, *packed),
            vmem(CHUNKS, XS, ZS, *packed),
            vmem(CHUNKS, 2, ZS, *packed),
            vmem(2, SLOTS, *packed),
            vmem(MB, SLOTS, TILE, LANES),
            dma((LAYERS,)),
            dma((MB,)),
        ]
        + [
            dma((CHUNKS, 2)), dma((CHUNKS,)), dma((CHUNKS,)), dma((CHUNKS,)),
            dma((CHUNKS, 2)), dma((CHUNKS,)), dma((CHUNKS,)), dma((CHUNKS,)), dma((2,)),
        ],
        compiler_params=pltpu.CompilerParams(
            has_side_effects=True, collective_id=0, vmem_limit_bytes=60 * 1024 * 1024
        ),
    )(source, weights, biases, inputs)
    return result[None]


def solution(mesh):
    in_specs = (
        P(None, "blk", None, None),
        P("segment", "blk", None, None),
        P("segment", "blk", None),
        P("segment", "blk", None),
    )
    out_specs = P("segment", "blk", None, None)
    return jax.shard_map(body, mesh=mesh, in_specs=in_specs, out_specs=out_specs, check_vma=False)
```

```python
import functools

import jax
import jax.numpy as jnp
from jax import lax
from jax.experimental import pallas as pl
from jax.experimental.pallas import tpu as pltpu
from jax.sharding import PartitionSpec as P

MESH = pl.DeviceIdType.MESH
TILE = 64
HALF = 32
FANIN = 32
LANES = 128
SLOTS = 16
ZS = 8
XS = 4
SEGS = 4
MB = 4
CHUNKS = 2 * MB
LAYERS = 2
ORDER = (("enter", 0), ("even", 0), ("spread", 1), ("odd", 2))
COLUMNS = FANIN // 2


def device(segment, x, z, core):
    return {"segment": segment, "blk": (x * ZS + z) * 2 + core}


def low_lanes(shape, width, period):
    lane = lax.broadcasted_iota(jnp.int32, shape, len(shape) - 1)
    return lax.rem(lane, period) < width


def repack(upper, lower):
    low = low_lanes(upper.shape, 64, 128)
    first = jnp.where(low, upper, pltpu.roll(lower, 64, upper.ndim - 1))
    second = jnp.where(low, pltpu.roll(upper, 64, upper.ndim - 1), lower)
    return first, second


def kernel(
    source, weights, bias_rows, inputs, out,
    raw_even, raw_odd, bias, near, far, entering, hidden, landed, odd_in, leaving, final, staged,
    raw_sem, in_sem, entry_recv, entry_send, core_recv, core_send, z_recv, z_send,
    x_recv, x_send, final_recv,
):
    raw = (raw_even, raw_odd)
    segment = lax.axis_index("segment")
    position = lax.axis_index("blk")
    x, z, core = position // (2 * ZS), position // 2 % ZS, position % 2
    upper, inner = x // 2, x % 2
    pair = device(segment, x, z, 1 - core)
    last = segment == SEGS - 1
    first = segment == 0

    def remote(src, dst, send, recv, target):
        return pltpu.make_async_remote_copy(
            src_ref=src, dst_ref=dst, send_sem=send, recv_sem=recv,
            device_id=target, device_id_type=MESH,
        )

    barrier = pltpu.get_barrier_semaphore()

    def greet(target):
        pl.semaphore_signal(barrier, inc=1, device_id=target, device_id_type=MESH)

    greet(pair)
    for step in (2, 1, 3):
        greet(device(segment, (x + step) % XS, z, core))
    for step in (4, 3, 5, 2, 6, 1, 7):
        greet(device(segment, x, (z + step) % ZS, core))

    @pl.when(segment > 0)
    def _():
        for step in (4, 3, 5, 2, 6, 1, 7, 0):
            for other in range(2):
                greet(device(segment - 1, 2 * upper + other, (z + step) % ZS, core))

    def raw_start(layer):
        for column in range(COLUMNS):
            pltpu.make_async_copy(
                weights.at[layer, :, :, pl.ds(column * LANES, LANES)],
                raw[layer].at[:, column], raw_sem.at[layer],
            ).start()

    def raw_copy(layer):
        return pltpu.make_async_copy(
            raw[layer].at[:, pl.ds(COLUMNS, COLUMNS)], raw[layer].at[:, pl.ds(0, COLUMNS)],
            raw_sem.at[layer],
        )

    def in_copy(batch):
        return pltpu.make_async_copy(inputs.at[batch], staged.at[batch], in_sem.at[batch])

    @pl.when(first)
    def _():
        for batch in range(MB):
            in_copy(batch).start()

    raw_start(0)
    raw_start(1)

    def arrange(layer):
        tiles = raw[layer]
        raw_copy(layer).wait()

        def turn(slot, carry):
            for column in range(COLUMNS):
                tiles[slot, COLUMNS + column] = pltpu.roll(tiles[slot, column], 64, 1)
            return carry

        lax.fori_loop(0, SLOTS, turn, 0)

        def one_slot(slot, carry):
            rows = pl.ds(pl.multiple_of(slot * TILE, TILE), TILE)
            low = low_lanes((TILE, LANES), 64, 128)
            quarter = low_lanes((TILE, LANES), 32, 64)
            ours = tiles.at[slot]

            def tile_at(member):
                return ours[source[layer, slot, member]]

            for quad in range(FANIN // 4):
                even = jnp.where(low, tile_at(4 * quad), tile_at(4 * quad + 2))
                odd = jnp.where(low, tile_at(4 * quad + 1), tile_at(4 * quad + 3))
                near[layer, quad, rows] = jnp.where(quarter, even, pltpu.roll(odd, 32, 1))
                far[layer, quad, rows] = jnp.where(quarter, pltpu.roll(even, 96, 1), odd)
            return carry

        lax.fori_loop(0, SLOTS, one_slot, 0)

    low = low_lanes((HALF, LANES), 64, 128)
    for layer in range(LAYERS):
        columns = jnp.transpose(bias_rows[layer], (1, 0))
        for slot in range(SLOTS):
            upper_half = jnp.broadcast_to(columns[:HALF, slot : slot + 1], (HALF, LANES))
            lower_half = jnp.broadcast_to(columns[HALF:, slot : slot + 1], (HALF, LANES))
            bias[layer, slot] = jnp.where(low, upper_half, lower_half)

    @pl.when(first)
    def _():
        for batch in range(MB):
            in_copy(batch).wait()

        def pack(step, carry):
            batch, block = step // SLOTS, step % SLOTS
            one, two = repack(
                staged[batch, block, pl.ds(0, HALF), :], staged[batch, block, pl.ds(HALF, HALF), :]
            )
            entering[2 * batch, core, block // ZS, block % ZS] = one
            entering[2 * batch + 1, core, block // ZS, block % ZS] = two
            return carry

        lax.fori_loop(0, MB * SLOTS, pack, 0)

    arrange(0)

    @pl.when(segment > 0)
    def _():
        arrange(1)

    pl.semaphore_wait(barrier, 11 + jnp.where(last, 0, 16))

    def joined(blocks, layer, rows):
        return jnp.concatenate([blocks[layer, quad, rows] for quad in range(FANIN // 4)], axis=1)

    def multiply(layer, values, block, store):
        rows = pl.ds(pl.multiple_of(block * 4 * TILE, 4 * TILE), 4 * TILE)
        one = jnp.dot(joined(near, layer, rows), values, preferred_element_type=jnp.float32)
        two = jnp.dot(joined(far, layer, rows), values, preferred_element_type=jnp.float32)
        for slot in range(4):
            a, b, c = slot * TILE, slot * TILE + HALF, (slot + 1) * TILE
            kept = jnp.where(low, one[a:b], two[b:c])
            moved = jnp.where(low, one[b:c], two[a:b])
            total = kept + pltpu.roll(moved, 64, 1) + bias[layer, block * 4 + slot]
            store(slot, jnp.maximum(total, 0.0).astype(jnp.bfloat16))

    def quarter_of(group):
        return pl.ds((z // 4 + 1 + group) % 2 * 4, 4)

    def core_copy(chunk, span):
        return remote(
            entering.at[chunk, core, :, span], entering.at[chunk, core, :, span],
            core_send.at[chunk], core_recv.at[chunk], pair,
        )

    def entry_done(chunk, group):
        span = pl.ds(0, 4)
        return remote(
            leaving.at[chunk, :, span], entering.at[chunk, core, :, span],
            entry_send.at[chunk], entry_recv.at[chunk, group], pair,
        )

    def z_done(chunk, group, count):
        span = pl.ds(0, count)
        return remote(
            hidden.at[chunk, :, span], landed.at[chunk, :, span],
            z_send.at[chunk], z_recv.at[chunk, group], pair,
        )

    def x_done(chunk):
        span = pl.ds(0, XS - 1)
        return remote(
            odd_in.at[chunk, span], odd_in.at[chunk, span],
            x_send.at[chunk], x_recv.at[chunk], pair,
        )

    @pl.when(first)
    def _():
        for chunk in range(CHUNKS):
            core_copy(chunk, pl.ds(0, ZS)).start()

    def enter(chunk):
        @pl.when(segment > 0)
        def _():
            for group in range(2):
                entry_done(chunk, group).wait_recv()
                core_copy(chunk, quarter_of(group)).start()

    def even_layer(chunk):
        core_copy(chunk, pl.ds(0, ZS)).wait_recv()
        values = entering[chunk].reshape(FANIN * HALF, LANES)
        for group in range(2):
            part = (z // 4 + 1 + group) % 2
            for other in range(2):
                def store(slot, block):
                    hidden[chunk, other, part * 4 + slot] = block

                multiply(0, values, 2 * other + part, store)
            for step in range(4):
                to = part * 4 + step

                @pl.when(to != z)
                def _():
                    remote(
                        hidden.at[chunk, :, to], landed.at[chunk, :, z],
                        z_send.at[chunk], z_recv.at[chunk, group],
                        device(segment, x, to, core),
                    ).start()

    def spread(chunk):
        for group in range(2):
            z_done(chunk, group, 4 - group).wait_recv()
            if group == 1:
                landed[chunk, :, z] = hidden[chunk, :, z]
            span = quarter_of(group)
            for step in (2, 1, 3):
                to = (x + step) % XS
                remote(
                    landed.at[chunk, to % 2, span], odd_in.at[chunk, x, span],
                    x_send.at[chunk], x_recv.at[chunk], device(segment, to, z, core),
                ).start()
        odd_in[chunk, x] = landed[chunk, inner]

    def odd_layer(chunk):
        x_done(chunk).wait_recv()
        values = odd_in[chunk].reshape(FANIN * HALF, LANES)
        goal = chunk // 2
        for group in range(2):
            part = (z // 4 + 1 + group) % 2
            for other in range(2):
                def store(slot, block):
                    leaving[chunk, other, part * 4 + slot] = block

                multiply(1, values, 2 * other + part, store)
                for step in range(4):
                    to = part * 4 + step
                    block = leaving.at[chunk, other, to]

                    @pl.when(segment < SEGS - 1)
                    def _():
                        remote(
                            block, entering.at[chunk, core, inner, z],
                            entry_send.at[chunk], entry_recv.at[chunk, group],
                            device(segment + 1, 2 * upper + other, to, core),
                        ).start()

                    @pl.when(last)
                    def _():
                        stays = (goal == SEGS - 1) & (to == z) & (other == inner)

                        @pl.when(jnp.logical_not(stays))
                        def _():
                            remote(
                                block, final.at[chunk % 2, inner * ZS + z],
                                entry_send.at[chunk], final_recv.at[chunk % 2],
                                device(goal, 2 * upper + other, to, core),
                            ).start()

        @pl.when(last & (goal == SEGS - 1))
        def _():
            final[chunk % 2, inner * ZS + z] = leaving[chunk, inner, z]

    phases = {"enter": enter, "even": even_layer, "spread": spread, "odd": odd_layer}

    def step(index, carry):
        for name, lag in ORDER:
            chunk = index - lag

            @pl.when((chunk >= 0) & (chunk < CHUNKS))
            def _():
                phases[name](chunk)

            if name == "even":
                @pl.when(first & (chunk == 0))
                def _():
                    arrange(1)

        return carry

    lax.fori_loop(0, CHUNKS + max(lag for _, lag in ORDER), step, 0)

    def final_done(half, count):
        span = pl.ds(0, count)
        return remote(
            final.at[half, span], final.at[half, span],
            entry_send.at[half], final_recv.at[half], pair,
        )

    @pl.when(segment < SEGS - 1)
    def _():
        for half in range(2):
            final_done(half, SLOTS).wait_recv()

    @pl.when(last)
    def _():
        for half in range(2):
            final_done(half, SLOTS - 1).wait_recv()

    def unpack(block, carry):
        one, two = repack(final[0, block], final[1, block])
        out[block, pl.ds(0, HALF), :] = one
        out[block, pl.ds(HALF, HALF), :] = two
        return carry

    lax.fori_loop(0, SLOTS, unpack, 0)

    def drain(chunk, carry):
        core_copy(chunk, pl.ds(0, ZS)).wait_send()
        z_done(chunk, 0, ZS - 1).wait_send()
        x_done(chunk).wait_send()
        whole = jnp.logical_not(last & (chunk // 2 == SEGS - 1))

        @pl.when(whole)
        def _():
            span = pl.ds(0, SLOTS)
            remote(
                final.at[0, span], final.at[0, span],
                entry_send.at[chunk], final_recv.at[0], pair,
            ).wait_send()

        @pl.when(jnp.logical_not(whole))
        def _():
            span = pl.ds(0, SLOTS - 1)
            remote(
                final.at[0, span], final.at[0, span],
                entry_send.at[chunk], final_recv.at[0], pair,
            ).wait_send()

        return carry

    lax.fori_loop(0, CHUNKS, drain, 0)


def body(inputs, weights, biases, tile_index):
    order = jnp.arange(FANIN, dtype=jnp.int32)
    high = (order // 2) % 2
    place = (order[:, None] + high) % 2 * COLUMNS + order[:, None] // 2
    source = jnp.sum(
        jnp.where(tile_index[..., :, None] == order, place, 0), axis=-2, dtype=jnp.int32
    )
    dma = pltpu.SemaphoreType.DMA
    packed = (HALF, LANES)
    vmem = lambda *shape: pltpu.VMEM(shape, jnp.bfloat16)
    result = pl.pallas_call(
        kernel,
        out_shape=jax.ShapeDtypeStruct((SLOTS, TILE, LANES), jnp.bfloat16),
        in_specs=[
            pl.BlockSpec(memory_space=pltpu.SMEM),
            pl.BlockSpec(memory_space=pl.ANY),
            pl.BlockSpec(memory_space=pltpu.VMEM),
            pl.BlockSpec(memory_space=pl.ANY),
        ],
        out_specs=pl.BlockSpec(memory_space=pltpu.VMEM),
        scratch_shapes=[
            vmem(SLOTS, 2 * COLUMNS, TILE, LANES),
            vmem(SLOTS, 2 * COLUMNS, TILE, LANES),
            pltpu.VMEM((LAYERS, SLOTS, HALF, LANES), jnp.float32),
            vmem(LAYERS, FANIN // 4, SLOTS * TILE, LANES),
            vmem(LAYERS, FANIN // 4, SLOTS * TILE, LANES),
            vmem(CHUNKS, 2, 2, ZS, *packed),
            vmem(CHUNKS, 2, ZS, *packed),
            vmem(CHUNKS, 2, ZS, *packed),
            vmem(CHUNKS, XS, ZS, *packed),
            vmem(CHUNKS, 2, ZS, *packed),
            vmem(2, SLOTS, *packed),
            vmem(MB, SLOTS, TILE, LANES),
            dma((LAYERS,)),
            dma((MB,)),
        ]
        + [
            dma((CHUNKS, 2)), dma((CHUNKS,)), dma((CHUNKS,)), dma((CHUNKS,)),
            dma((CHUNKS, 2)), dma((CHUNKS,)), dma((CHUNKS,)), dma((CHUNKS,)), dma((2,)),
        ],
        compiler_params=pltpu.CompilerParams(
            has_side_effects=True, collective_id=0, vmem_limit_bytes=60 * 1024 * 1024
        ),
    )(source, weights, biases, inputs)
    return result[None]


def solution(mesh):
    in_specs = (
        P(None, "blk", None, None),
        P("segment", "blk", None, None),
        P("segment", "blk", None),
        P("segment", "blk", None),
    )
    out_specs = P("segment", "blk", None, None)
    return jax.shard_map(body, mesh=mesh, in_specs=in_specs, out_specs=out_specs, check_vma=False)
```
